32 devices in a mesh: sp: 4 (over z), bn: 2 (over x), dp: 4 (over y, core).
Axes of the slice: x: 2, y: 2, z: 4, core: 2. Of those that a mesh axis runs over, the one named last changes fastest.
Arguments:
- images: bfloat16 [8, 4, 64, 40, 128], P(('bn', 'dp'), 'sp'), may hold values from -8 to 8, as said below
- out_grad: bfloat16 [8, 4, 256, 40, 128], P(('bn', 'dp'), 'sp'), may hold values from -8 to 8, as said below
- conv_weight: bfloat16 [3, 3, 64, 64], replicated, may hold values from -0.25 to 0.25
- proj_weight: bfloat16 [64, 256], replicated, may hold values from -0.75 to 0.75
- gain_one: float32 [64], replicated, may hold values from 0.1 to 1.9
- shift_one: float32 [64], replicated, may hold values from -3 to 3
- gain_three: float32 [256], replicated, may hold values from 0.1 to 1.9
- shift_three: float32 [256], replicated, may hold values from -3 to 3
Outputs:
- images_grad: bfloat16 [8, 4, 64, 40, 128], P(('bn', 'dp'), 'sp')
- conv_grad: float32 [3, 3, 64, 64], replicated
- proj_grad: float32 [64, 256], replicated
- gain_one_grad: float32 [64], replicated
- shift_one_grad: float32 [64], replicated
- gain_three_grad: float32 [256], replicated
- shift_three_grad: float32 [256], replicated
The draws below stay inside these ranges and needn't reach their ends.
Inputs may be any that keep to these rules, and one draw needn't show every extreme that they name: `images`: channels of one quadrant have their own offset and spread. `out_grad`: channels of one quadrant have their own offset and spread.
All inputs are finite; a program needn't handle non-finite values.
Results may differ from the reference program's by a relative error of at most 0.029.
Values may be sent and summed in bfloat16 or wider, within the bound.
A program may use at most 64 MiB of HBM per device.

```python
import jax
import jax.numpy as jnp
from jax import lax

C = 64
CO = 256
TH = 40
TW = 128
IMG_DEV = 1
IMAGES = 8
N_BN = 2
N_DP = 4


def tile_draw(key, channels, salt_value):
    folded = jax.random.fold_in(key, salt_value)
    subkeys = jax.random.split(folded, 4)
    corner = (IMAGES, 4, channels, 1, 1)
    whole = (IMAGES, 4, channels, TH, TW)
    offsets = 1.5 * jax.random.normal(subkeys[0], corner, jnp.float32)
    spreads = jnp.exp(jax.random.uniform(subkeys[1], corner, jnp.float32, -1.2, 0.5))
    jitter = jax.random.normal(subkeys[2], whole, jnp.float32)
    drawn = offsets + spreads * jitter
    return jnp.clip(drawn, -8.0, 8.0)


def draw_images(key, part):
    return tile_draw(key, C, 3).astype(jnp.bfloat16)


def draw_out_grad(key, part):
    return tile_draw(key, CO, 7).astype(jnp.bfloat16)


def noise(stream_key, extent, scale, bound, held_as=jnp.bfloat16):
    return jnp.clip(scale * jax.random.normal(stream_key, extent, jnp.float32), -bound, bound).astype(held_as)


def setup_inputs(seed: int = 0) -> dict:
    key_of = jax.random.split(jax.random.key(seed), 9)
    return {
        "images": draw_images(jax.random.fold_in(key_of[8], 71), 0),
        "out_grad": draw_out_grad(jax.random.fold_in(key_of[8], 71), 0),
        "conv_weight": noise(key_of[2], (3, 3, C, C), (9 * C) ** -0.5, 0.25),
        "proj_weight": noise(key_of[3], (C, CO), C ** -0.5, 0.75),
        "gain_one": jnp.clip(1.0 + 0.18 * jax.random.normal(key_of[4], (C,), jnp.float32), 0.1, 1.9),
        "shift_one": noise(key_of[5], (C,), 1.0, 3.0, jnp.float32),
        "gain_three": jnp.clip(1.0 + 0.18 * jax.random.normal(key_of[6], (CO,), jnp.float32), 0.1, 1.9),
        "shift_three": noise(key_of[7], (CO,), 1.0, 3.0, jnp.float32),
    }


norm_floor = 1e-05

def silu_slope(inputs):
    sigma = jax.nn.sigmoid(inputs)
    return sigma * (1.0 + inputs * (1.0 - sigma))

def channel(vector):
    return vector[None, :, None, None]

def assemble(tiles):
    groups, quadrants, depth, tile_rows, tile_cols = tiles.shape
    merged = tiles.reshape(groups, 2, 2, depth, tile_rows, tile_cols)
    return merged.transpose(0, 3, 1, 4, 2, 5).reshape(groups, depth, 2 * tile_rows, 2 * tile_cols)

def split_back(field):
    groups, depth, height, breadth = field.shape
    parted = field.reshape(groups, depth, 2, height // 2, 2, breadth // 2)
    return parted.transpose(0, 2, 4, 1, 3, 5).reshape(groups, 4, depth, height // 2, breadth // 2)

def shifted(padded, start_row, start_col, height, breadth):
    return padded[:, :, start_row:start_row + height, start_col:start_col + breadth].astype(jnp.float32)

def pad_cells(field):
    return jnp.pad(field, ((0, 0), (0, 0), (1, 1), (1, 1)))

def moments(values):
    average = lax.optimization_barrier(jnp.mean(values, axis=(0, 2, 3)))
    centred = values - channel(average)
    return (average, lax.optimization_barrier(jnp.mean(centred * centred, axis=(0, 2, 3))))

def group_pass(image_tiles, cot_tiles, conv_weight, proj_weight, gain_one, shift_one, gain_three, shift_three):
    field = assemble(image_tiles)
    cotangent = assemble(cot_tiles)
    height = field.shape[2]
    breadth = field.shape[3]
    cell_count = field.shape[0] * height * breadth
    padded = pad_cells(field)
    kernel = conv_weight.astype(jnp.float32)
    conv_out = None
    for row_off in range(3):
        for col_off in range(3):
            partial_sum = jnp.einsum('oi,gihw->gohw', kernel[row_off, col_off], shifted(padded, row_off, col_off, height, breadth))
            conv_out = partial_sum if conv_out is None else conv_out + partial_sum
    mean_one, var_one = moments(conv_out)
    scale_one = lax.rsqrt(var_one + norm_floor)
    normed_one = (conv_out - channel(mean_one)) * channel(scale_one)
    before_act = channel(gain_one) * normed_one + channel(shift_one)
    hidden = jax.nn.silu(before_act).astype(jnp.bfloat16)
    hidden_float = hidden.astype(jnp.float32)
    project = proj_weight.astype(jnp.float32)
    widened = jnp.einsum('io,gihw->gohw', project, hidden_float)
    mean_three, var_three = moments(widened)
    scale_three = lax.rsqrt(var_three + norm_floor)
    normed_three = (widened - channel(mean_three)) * channel(scale_three)
    output_pre = channel(gain_three) * normed_three + channel(shift_three)
    grad_out = cotangent.astype(jnp.float32) * silu_slope(output_pre)
    sum_three = lax.optimization_barrier(jnp.sum(grad_out, axis=(0, 2, 3)))
    cross_three = lax.optimization_barrier(jnp.sum(grad_out * normed_three, axis=(0, 2, 3)))
    grad_wide = channel(gain_three * scale_three) * (grad_out - channel(sum_three) / cell_count - normed_three * channel(cross_three) / cell_count)
    grad_wide = grad_wide.astype(jnp.bfloat16).astype(jnp.float32)
    grad_proj = jnp.einsum('gihw,gohw->io', hidden_float, grad_wide)
    grad_hidden = jnp.einsum('io,gohw->gihw', project, grad_wide)
    grad_pre = grad_hidden * silu_slope(before_act)
    sum_one = lax.optimization_barrier(jnp.sum(grad_pre, axis=(0, 2, 3)))
    cross_one = lax.optimization_barrier(jnp.sum(grad_pre * normed_one, axis=(0, 2, 3)))
    grad_conv_out = channel(gain_one * scale_one) * (grad_pre - channel(sum_one) / cell_count - normed_one * channel(cross_one) / cell_count)
    grad_conv_out = grad_conv_out.astype(jnp.bfloat16)
    back_float = grad_conv_out.astype(jnp.float32)
    pieces_list = []
    for row_off in range(3):
        for col_off in range(3):
            pieces_list.append(jnp.einsum('gohw,gihw->oi', back_float, shifted(padded, row_off, col_off, height, breadth)))
    grad_kernel = jnp.stack(pieces_list).reshape(kernel.shape)
    back_pad = pad_cells(grad_conv_out)
    grad_field = None
    for row_off in range(3):
        for col_off in range(3):
            partial_sum = jnp.einsum('oi,gohw->gihw', kernel[row_off, col_off], shifted(back_pad, 2 - row_off, 2 - col_off, height, breadth))
            grad_field = partial_sum if grad_field is None else grad_field + partial_sum
    return (split_back(grad_field.astype(jnp.bfloat16)), grad_kernel, grad_proj, cross_one, sum_one, cross_three, sum_three)

def reference(images, out_grad, conv_weight, proj_weight, gain_one, shift_one, gain_three, shift_three):

    def regroup(tiles):
        depth = tiles.shape[2]
        sectioned = tiles.reshape(N_BN, N_DP, IMG_DEV, 4, depth, TH, TW).transpose(1, 0, 2, 3, 4, 5, 6)
        return sectioned.reshape(N_DP, N_BN * IMG_DEV, 4, depth, TH, TW)

    def one_group(inputs_pair):
        return group_pass(inputs_pair[0], inputs_pair[1], conv_weight, proj_weight, gain_one, shift_one, gain_three, shift_three)
    results = lax.map(one_group, (regroup(images), regroup(out_grad)))
    grad_tiles = results[0].reshape(N_DP, N_BN, IMG_DEV, 4, C, TH, TW).transpose(1, 0, 2, 3, 4, 5, 6)
    grad_tiles = grad_tiles.reshape(IMAGES, 4, C, TH, TW)
    per_image = 1.0 / (4 * TH * TW)
    return (grad_tiles, lax.optimization_barrier(jnp.sum(results[1], axis=0)) * per_image, lax.optimization_barrier(jnp.sum(results[2], axis=0)) * per_image, lax.optimization_barrier(jnp.sum(results[3], axis=0)) * per_image, lax.optimization_barrier(jnp.sum(results[4], axis=0)) * per_image, lax.optimization_barrier(jnp.sum(results[5], axis=0)) * per_image, lax.optimization_barrier(jnp.sum(results[6], axis=0)) * per_image)
```

```python
import functools

import jax
import jax.numpy as jnp
from jax import lax
from jax.experimental import pallas as pl
from jax.experimental.pallas import tpu as pltpu
from jax.sharding import PartitionSpec as P

norm_floor = 1e-05
F32 = jnp.float32
BF16 = jnp.bfloat16
MESH = pl.DeviceIdType.MESH
LANES = 128
NT = (((1,), (1,)), ((), ()))


def sig(v):
    return 0.5 * jnp.tanh(0.5 * v) + 0.5


def to_row(col):
    return jnp.broadcast_to(col, (col.shape[0], LANES)).T[0:1]


def to_col(row):
    return jnp.broadcast_to(row, (LANES, row.shape[1])).T


def pick(count, options):
    return next(o for o in options if count % o == 0)


def kernel(
    n_sp, n_bn, n_dp,
    x_ref, g_ref, wf_ref, wb_ref, wpt_ref, wp_ref, vec1_ref, vec3_ref,
    ig_ref, cg_out, pg_out, q1_out, s1_out, q3_out, s3_out,
    xs, ds, a_buf, e1_buf, b_buf, e3_buf, y_buf, acc, cgt, gpt,
    packed, halo, stats, rs_send, rs_recv, line, fin,
    h_send, h_recv, st_send, st_recv, rs_ss, rs_rs, ln_ss, ln_rs, ag_ss, ag_rs,
):
    th, c, tw = x_ref.shape
    co = g_ref.shape[1]
    n_grp = n_sp * n_bn
    n_pl = n_bn * n_dp
    shard = line.shape[1]
    local_cells = float(th * tw)
    cells = local_cells * n_grp
    factor = 1.0 / (n_sp * local_cells)
    sp = lax.axis_index("sp")
    bn = lax.axis_index("bn")
    dp = lax.axis_index("dp")
    col = sp % 2
    rh = sp // 2
    me_g = sp * n_bn + bn
    me_p = bn * n_dp + dp

    def group_peer(d):
        p = (me_g + d) % n_grp
        return {"sp": p // n_bn, "bn": p % n_bn, "dp": dp}

    def plane_peer(d):
        p = (me_p + d) % n_pl
        return p, {"sp": sp, "bn": p // n_dp, "dp": p % n_dp}

    def line_peer(d):
        return {"sp": (sp + d) % n_sp, "bn": bn, "dp": dp}

    barrier = pltpu.get_barrier_semaphore()

    def greet_group(d, carry):
        pl.semaphore_signal(barrier, inc=1, device_id=group_peer(d), device_id_type=MESH)
        return carry

    def greet_plane(d, carry):
        pl.semaphore_signal(barrier, inc=1, device_id=plane_peer(d)[1], device_id_type=MESH)
        return carry

    lax.fori_loop(1, n_grp, greet_group, 0)
    lax.fori_loop(1, n_pl, greet_plane, 0)

    lane = lax.broadcasted_iota(jnp.int32, (c, tw), 1)
    left = lane == 0
    right = lane == tw - 1
    edge = (tw - 1) * (1 - col)
    edge_row = (1 - rh) * (th - 1)
    is_c1 = col.astype(F32)
    is_c0 = 1.0 - is_c1

    def pack_cols(get):
        def step(h, got):
            turned = pltpu.roll(get(h), (h + tw - edge) % tw, 1)
            return jnp.where(lane == h, turned, got)

        return lax.fori_loop(0, th, step, jnp.zeros((c, tw), F32))

    def halo_copies(k, row_src):
        out = []
        for s, (src, flip) in enumerate(((packed.at[k], 1), (row_src, 2), (row_src, 3))):
            pcol = col if flip == 2 else 1 - col
            prow = rh if flip == 1 else 1 - rh
            out.append(
                pltpu.make_async_remote_copy(
                    src_ref=src, dst_ref=halo.at[k, s], send_sem=h_send.at[k, s], recv_sem=h_recv.at[k, s],
                    device_id={"sp": prow * 2 + pcol, "bn": bn, "dp": dp}, device_id_type=MESH,
                )
            )
        return out

    def fill(dst, k, get):
        got = halo[k, 0].astype(F32)

        def step(h, carry):
            v = get(h)
            edge_col = pltpu.roll(got, (edge + tw - h) % tw, 1)
            dst[h + 1, 0:c] = jnp.where(left, edge_col * is_c1, pltpu.roll(v, 1, 1)).astype(BF16)
            dst[h + 1, c : 2 * c] = v.astype(BF16)
            dst[h + 1, 2 * c : 3 * c] = jnp.where(right, edge_col * is_c0, pltpu.roll(v, tw - 1, 1)).astype(BF16)
            return carry

        lax.fori_loop(0, th, step, 0)
        v = halo[k, 1].astype(F32)
        diag = halo[k, 2].astype(F32)
        real = (1 - rh) * (th + 1)
        dst[real, 0:c] = jnp.where(left, pltpu.roll(diag, 1, 1) * is_c1, pltpu.roll(v, 1, 1)).astype(BF16)
        dst[real, c : 2 * c] = v.astype(BF16)
        dst[real, 2 * c : 3 * c] = jnp.where(
            right, pltpu.roll(diag, tw - 1, 1) * is_c0, pltpu.roll(v, tw - 1, 1)
        ).astype(BF16)
        dst[rh * (th + 1)] = jnp.zeros((3 * c, tw), BF16)

    def exchange(k, first, second):
        n = first.shape[1]
        stats[k, me_g, 0:1, 0:n] = first
        stats[k, me_g, 1:2, 0:n] = second

        def copy_to(d):
            return pltpu.make_async_remote_copy(
                src_ref=stats.at[k, me_g], dst_ref=stats.at[k, me_g],
                send_sem=st_send.at[k, d], recv_sem=st_recv.at[k, d],
                device_id=group_peer(d), device_id_type=MESH,
            )

        def start(d, carry):
            copy_to(d).start()
            return carry

        def finish(d, carry):
            src = (me_g + n_grp - d) % n_grp
            arrival = pltpu.make_async_remote_copy(
                src_ref=stats.at[k, me_g], dst_ref=stats.at[k, src],
                send_sem=st_send.at[k, d], recv_sem=st_recv.at[k, d],
                device_id=group_peer(d), device_id_type=MESH,
            )
            arrival.wait_recv()
            arrival.wait_send()
            return carry

        lax.fori_loop(1, n_grp, start, 0)
        lax.fori_loop(1, n_grp, finish, 0)
        firsts = [stats[k, j, 0:1, 0:n] for j in range(n_grp)]
        seconds = [stats[k, j, 1:2, 0:n] for j in range(n_grp)]
        return firsts, seconds

    def moments(k, mean_row, square_row):
        means, squares = exchange(k, mean_row, square_row)
        mean = sum(means[1:], means[0]) / float(n_grp)
        square = sum(squares[1:], squares[0])
        for m in means:
            square = square + local_cells * (m - mean) * (m - mean)
        return mean, square / cells

    def sums(k, first, second):
        a, b = exchange(k, first, second)
        return sum(a[1:], a[0]), sum(b[1:], b[0])

    def row_sum(v):
        return jnp.sum(v.T, axis=0, keepdims=True)

    get_x = lambda h: x_ref[h].astype(F32)
    packed[0] = pack_cols(get_x).astype(BF16)
    pl.semaphore_wait(barrier, n_grp - 1 + n_pl - 1)
    x_copies = halo_copies(0, x_ref.at[edge_row])
    for copy in x_copies:
        copy.start()
    for copy in x_copies:
        copy.wait()
    fill(xs, 0, get_x)

    r4 = pick(th, (4, 2, 1))
    r8 = pick(th, (8, 4, 2, 1))
    r2 = pick(th, (2, 1))

    def columns(src, h, r):
        return jnp.concatenate([src[pl.ds(h + k, 3)].reshape(9 * c, tw) for k in range(r)], axis=1)

    def conv_step(t, got):
        h = t * r4
        res = jnp.dot(wf_ref[...], columns(xs, h, r4), preferred_element_type=F32)
        for k in range(r4):
            piece = res[:, k * tw : (k + 1) * tw]
            a_buf[h + k] = piece
            got = got + piece
        return got

    zero_c = jnp.zeros((c, tw), F32)
    total = lax.fori_loop(0, th // r4, conv_step, zero_c)
    mean_col = jnp.sum(total, axis=1, keepdims=True) / local_cells

    def square_step(h, got):
        d = a_buf[h] - mean_col
        return got + d * d

    sq = lax.fori_loop(0, th, square_step, zero_c)
    mu1, var1 = moments(0, to_row(mean_col), row_sum(sq))
    s1 = lax.rsqrt(var1 + norm_floor)
    gain1 = vec1_ref[0:1]
    mu1_c = to_col(mu1)
    s1_c = to_col(s1)
    gain1_c = to_col(gain1)
    shift1_c = to_col(vec1_ref[1:2])

    acc[...] = jnp.zeros_like(acc)

    def wide_step(t, carry):
        h = t * r2
        parts = []
        for k in range(r2):
            n1 = (a_buf[h + k] - mu1_c) * s1_c
            a_buf[h + k] = n1
            p1 = gain1_c * n1 + shift1_c
            parts.append((p1 * sig(p1)).astype(BF16))
        y = jnp.concatenate(parts, axis=1)
        y_buf[:, pl.ds(pl.multiple_of(h * tw, tw), r2 * tw)] = y
        res = jnp.dot(wpt_ref[...], y, preferred_element_type=F32)
        more = None
        for k in range(r2):
            piece = res[:, k * tw : (k + 1) * tw]
            b_buf[h + k] = piece
            more = piece if more is None else more + piece
        acc[...] += more
        return carry

    lax.fori_loop(0, th // r2, wide_step, 0)
    mean3_col = jnp.sum(acc[...], axis=1, keepdims=True) / local_cells
    sq_rows = []
    for j in range(0, co, c):
        m = jnp.broadcast_to(mean3_col[j : j + c], (c, tw))

        def square3(h, got, j=j, m=m):
            d = b_buf[h, j : j + c] - m
            return got + d * d

        sq_rows.append(row_sum(lax.fori_loop(0, th, square3, zero_c, unroll=2)))
    mu3, var3 = moments(1, to_row(mean3_col), jnp.concatenate(sq_rows, axis=1))
    s3 = lax.rsqrt(var3 + norm_floor)
    gain3 = vec3_ref[0:1]
    mu3_c = to_col(mu3)
    s3_c = to_col(s3)
    gain3_c = to_col(gain3)
    shift3_c = to_col(vec3_ref[1:2])

    sum_rows, cross_rows = [], []
    for j in range(0, co, c):
        mu_j = mu3_c[j : j + c]
        s_j = s3_c[j : j + c]
        g_j = gain3_c[j : j + c]
        b_j = shift3_c[j : j + c]

        def out_step(h, got, j=j, mu_j=mu_j, s_j=s_j, g_j=g_j, b_j=b_j):
            n3 = (b_buf[h, j : j + c] - mu_j) * s_j
            p3 = g_j * n3 + b_j
            g = sig(p3)
            e3 = g_ref[h, j : j + c].astype(F32) * (g * (1.0 + p3 * (1.0 - g)))
            b_buf[h, j : j + c] = n3
            e3_buf[h, j : j + c] = e3
            return got[0] + e3, got[1] + e3 * n3

        ssum, scross = lax.fori_loop(0, th, out_step, (zero_c, zero_c))
        sum_rows.append(row_sum(ssum))
        cross_rows.append(row_sum(scross))
    local_s3 = jnp.concatenate(sum_rows, axis=1)
    local_q3 = jnp.concatenate(cross_rows, axis=1)
    full_s3, full_q3 = sums(2, local_s3, local_q3)
    coef_a = to_col(gain3 * s3)
    coef_s = to_col(full_s3 / cells)
    coef_q = to_col(full_q3 / cells)

    gpt[...] = jnp.zeros_like(gpt)

    def back_step(t, got):
        h = t * r2
        parts = []
        for k in range(r2):
            pieces = []
            for j in range(0, co, c):
                q = slice(j, j + c)
                db = coef_a[q] * (e3_buf[h + k, q] - coef_s[q] - b_buf[h + k, q] * coef_q[q])
                pieces.append(db.astype(BF16))
            parts.append(jnp.concatenate(pieces, axis=0))
        db = jnp.concatenate(parts, axis=1)
        y = y_buf[:, pl.ds(pl.multiple_of(h * tw, tw), r2 * tw)]
        gpt[...] += lax.dot_general(db, y, NT, preferred_element_type=F32)
        gh = jnp.dot(wp_ref[...], db, preferred_element_type=F32)
        ssum, scross = got
        for k in range(r2):
            n1 = a_buf[h + k]
            p1 = gain1_c * n1 + shift1_c
            g = sig(p1)
            e1 = gh[:, k * tw : (k + 1) * tw] * (g * (1.0 + p1 * (1.0 - g)))
            e1_buf[h + k] = e1
            ssum = ssum + e1
            scross = scross + e1 * n1
        return ssum, scross

    ssum, scross = lax.fori_loop(0, th // r2, back_step, (zero_c, zero_c))
    local_s1 = row_sum(ssum)
    local_q1 = row_sum(scross)
    full_s1, full_q1 = sums(3, local_s1, local_q1)
    d_a = to_col(gain1 * s1)
    d_s = to_col(full_s1 / cells)
    d_q = to_col(full_q1 / cells)

    def da_step(h, got):
        da = (d_a * (e1_buf[h] - d_s - a_buf[h] * d_q)).astype(BF16)
        ds[h + 1, c : 2 * c] = da
        turned = pltpu.roll(da.astype(F32), (h + tw - edge) % tw, 1)
        return jnp.where(lane == h, turned, got)

    packed[1] = lax.fori_loop(0, th, da_step, zero_c).astype(BF16)
    d_copies = halo_copies(1, ds.at[edge_row + 1, pl.ds(c, c)])
    for copy in d_copies:
        copy.start()

    cgt[...] = jnp.zeros_like(cgt)

    def grad_step(t, carry):
        h = t * r8
        da = jnp.concatenate([ds[h + k + 1, c : 2 * c] for k in range(r8)], axis=1)
        cgt[...] += lax.dot_general(columns(xs, h, r8), da, NT, preferred_element_type=F32)
        return carry

    lax.fori_loop(0, th // r8, grad_step, 0)
    half = 9 * c // 2
    flat = jnp.concatenate([cgt[k * c : (k + 1) * c, :].T for k in range(9)], axis=0)
    rs_send[0:half] = jnp.concatenate([flat[:half], flat[half:]], axis=1)
    gp = gpt[...].T
    base = half
    for k in range(co // LANES):
        rs_send[base : base + c] = gp[:, k * LANES : (k + 1) * LANES]
        base += c
    rs_send[base:] = jnp.zeros((rs_send.shape[0] - base, LANES), F32)
    rs_send[base : base + 1] = jnp.concatenate([local_q1, local_s1], axis=1)
    small = base + 1
    for v in (local_q3, local_s3):
        for k in range(co // LANES):
            rs_send[small : small + 1] = v[:, k * LANES : (k + 1) * LANES]
            small += 1

    def span(p):
        return pl.ds(pl.multiple_of(p * shard, 8), shard)

    def rs_copy(d):
        p, where = plane_peer(d)
        return pltpu.make_async_remote_copy(
            src_ref=rs_send.at[span(p)], dst_ref=rs_recv.at[d], send_sem=rs_ss.at[d], recv_sem=rs_rs.at[d],
            device_id=where, device_id_type=MESH,
        )

    def rs_start(d, carry):
        rs_copy(d).start()
        return carry

    lax.fori_loop(1, n_pl, rs_start, 0)
    for copy in d_copies:
        copy.wait()

    fill(ds, 1, lambda h: ds[h + 1, c : 2 * c].astype(F32))

    def field_step(t, carry):
        h = t * r4
        res = jnp.dot(wb_ref[...], columns(ds, h, r4), preferred_element_type=F32)
        for k in range(r4):
            ig_ref[h + k] = res[:, k * tw : (k + 1) * tw].astype(BF16)
        return carry

    lax.fori_loop(0, th // r4, field_step, 0)

    def rs_wait(d, got):
        rs_copy(d).wait()
        return got + rs_recv[d]

    line[sp] = lax.fori_loop(1, n_pl, rs_wait, rs_send[span(me_p)])

    def ln_copy(d, slot):
        return pltpu.make_async_remote_copy(
            src_ref=line.at[sp], dst_ref=line.at[slot], send_sem=ln_ss.at[d], recv_sem=ln_rs.at[d],
            device_id=line_peer(d), device_id_type=MESH,
        )

    for d in range(1, n_sp):
        ln_copy(d, sp).start()
    for d in range(1, n_sp):
        ln_copy(d, (sp + n_sp - d) % n_sp).wait()
    whole = line[0]
    for k in range(1, n_sp):
        whole = whole + line[k]
    fin[span(me_p)] = whole * factor

    def ag_copy(d, slot):
        return pltpu.make_async_remote_copy(
            src_ref=fin.at[span(me_p)], dst_ref=fin.at[span(slot)], send_sem=ag_ss.at[d], recv_sem=ag_rs.at[d],
            device_id=plane_peer(d)[1], device_id_type=MESH,
        )

    def ag_start(d, carry):
        ag_copy(d, me_p).start()
        return carry

    def ag_wait(d, carry):
        ag_copy(d, (me_p + n_pl - d) % n_pl).wait()
        return carry

    lax.fori_loop(1, n_pl, ag_start, 0)
    lax.fori_loop(1, n_pl, ag_wait, 0)
    cg_out[0:half] = fin[0:half, 0:c]
    cg_out[half:] = fin[0:half, c : 2 * c]
    base = half
    for k in range(co // LANES):
        pg_out[:, k * LANES : (k + 1) * LANES] = fin[base : base + c]
        base += c
    q1_out[...] = fin[base : base + 1, 0:c]
    s1_out[...] = fin[base : base + 1, c : 2 * c]
    small = base + 1
    for ref in (q3_out, s3_out):
        for k in range(co // LANES):
            ref[:, k * LANES : (k + 1) * LANES] = fin[small : small + 1]
            small += 1


def shards(images, out_grad, conv_weight, proj_weight, gain_one, shift_one, gain_three, shift_three):
    _, _, c, th, tw = images.shape
    co = out_grad.shape[2]
    n_sp, n_bn, n_dp = (lax.axis_size(a) for a in ("sp", "bn", "dp"))
    n_grp, n_pl = n_sp * n_bn, n_bn * n_dp
    x = images[0, 0].transpose(1, 0, 2)
    g = out_grad[0, 0].transpose(1, 0, 2)
    wf = conv_weight.transpose(2, 0, 1, 3).reshape(c, 9 * c)
    wb = conv_weight[::-1, ::-1].transpose(3, 0, 1, 2).reshape(c, 9 * c)
    rows = 9 * c // 2 + c * (co // LANES) + 1 + 2 * (co // LANES)
    shard = 8 * (-(-rows // (8 * n_pl)))
    vm = pl.BlockSpec(memory_space=pltpu.VMEM)
    dma = pltpu.SemaphoreType.DMA
    outs = pl.pallas_call(
        functools.partial(kernel, n_sp, n_bn, n_dp),
        out_shape=(
            jax.ShapeDtypeStruct((th, c, tw), BF16),
            jax.ShapeDtypeStruct((9 * c, c), F32),
            jax.ShapeDtypeStruct((c, co), F32),
            jax.ShapeDtypeStruct((1, c), F32),
            jax.ShapeDtypeStruct((1, c), F32),
            jax.ShapeDtypeStruct((1, co), F32),
            jax.ShapeDtypeStruct((1, co), F32),
        ),
        in_specs=[vm] * 8,
        out_specs=(vm,) * 7,
        scratch_shapes=[
            pltpu.VMEM((th + 2, 3 * c, tw), BF16),
            pltpu.VMEM((th + 2, 3 * c, tw), BF16),
            pltpu.VMEM((th, c, tw), F32),
            pltpu.VMEM((th, c, tw), F32),
            pltpu.VMEM((th, co, tw), F32),
            pltpu.VMEM((th, co, tw), F32),
            pltpu.VMEM((c, th * tw), BF16),
            pltpu.VMEM((co, tw), F32),
            pltpu.VMEM((9 * c, c), F32),
            pltpu.VMEM((co, c), F32),
            pltpu.VMEM((2, c, tw), BF16),
            pltpu.VMEM((2, 3, c, tw), BF16),
            pltpu.VMEM((4, n_grp, 8, co), F32),
            pltpu.VMEM((n_pl * shard, LANES), F32),
            pltpu.VMEM((n_pl, shard, LANES), F32),
            pltpu.VMEM((n_sp, shard, LANES), F32),
            pltpu.VMEM((n_pl * shard, LANES), F32),
            dma((2, 3)), dma((2, 3)),
            dma((4, n_grp)), dma((4, n_grp)),
            dma((n_pl,)), dma((n_pl,)),
            dma((n_sp,)), dma((n_sp,)),
            dma((n_pl,)), dma((n_pl,)),
        ],
        compiler_params=pltpu.CompilerParams(
            collective_id=0, has_side_effects=True, vmem_limit_bytes=60 * 1024 * 1024
        ),
        name="branch_step",
    )(
        x, g, wf, wb, proj_weight.T, proj_weight,
        jnp.stack([gain_one, shift_one]), jnp.stack([gain_three, shift_three]),
    )
    ig, cg, pg, q1, s1, q3, s3 = outs
    return (
        ig.transpose(1, 0, 2)[None, None],
        cg.reshape(conv_weight.shape),
        pg, q1[0], s1[0], q3[0], s3[0],
    )


def solution(mesh):
    tiles = P(("bn", "dp"), "sp", None, None, None)
    return jax.shard_map(
        shards,
        mesh=mesh,
        in_specs=(tiles, tiles) + (P(),) * 6,
        out_specs=(tiles,) + (P(),) * 6,
        check_vma=False,
    )
```

```python
import functools

import jax
import jax.numpy as jnp
from jax import lax
from jax.experimental import pallas as pl
from jax.experimental.pallas import tpu as pltpu
from jax.sharding import PartitionSpec as P

norm_floor = 1e-05
F32 = jnp.float32
BF16 = jnp.bfloat16
MESH = pl.DeviceIdType.MESH
LANES = 128
NT = (((1,), (1,)), ((), ()))


def sig(v):
    return 0.5 * jnp.tanh(0.5 * v) + 0.5


def to_row(col):
    return jnp.broadcast_to(col, (col.shape[0], LANES)).T[0:1]


def to_col(row):
    return jnp.broadcast_to(row, (LANES, row.shape[1])).T


def pick(count, options):
    return next(o for o in options if count % o == 0)


def kernel(
    n_sp, n_bn, n_dp,
    x_hbm, g_hbm, cw_ref, wp_ref, gain1_ref, shift1_ref, gain3_ref, shift3_ref,
    ig_ref, fin,
    x_raw, g_raw, xf, gf, x_sem, g_sem, wf_ref, wb_ref, wpt_ref,
    xs, ds, a_buf, e1_buf, b_buf, e3_buf, y_buf, acc, cgt, gpt,
    packed, edge_x, halo, stats, rs_send, rs_recv, line,
    h_send, h_recv, st_send, st_recv, rs_ss, rs_rs, ln_ss, ln_rs, ag_ss, ag_rs,
):
    c, th, tw = x_raw.shape
    co = g_raw.shape[0]
    n_grp = n_sp * n_bn
    n_pl = n_bn * n_dp
    shard = line.shape[1]
    local_cells = float(th * tw)
    cells = local_cells * n_grp
    factor = 1.0 / (n_sp * local_cells)
    sp = lax.axis_index("sp")
    bn = lax.axis_index("bn")
    dp = lax.axis_index("dp")
    col = sp % 2
    rh = sp // 2
    me_g = sp * n_bn + bn
    me_p = bn * n_dp + dp

    def group_peer(d):
        p = (me_g + d) % n_grp
        return {"sp": p // n_bn, "bn": p % n_bn, "dp": dp}

    def plane_peer(d):
        p = (me_p + d) % n_pl
        return p, {"sp": sp, "bn": p // n_dp, "dp": p % n_dp}

    def line_peer(d):
        return {"sp": (sp + d) % n_sp, "bn": bn, "dp": dp}

    load_x = pltpu.make_async_copy(x_hbm, x_raw, x_sem)
    load_g = pltpu.make_async_copy(g_hbm, g_raw, g_sem)
    load_x.start()
    load_g.start()

    barrier = pltpu.get_barrier_semaphore()

    def greet_group(d, carry):
        pl.semaphore_signal(barrier, inc=1, device_id=group_peer(d), device_id_type=MESH)
        return carry

    def greet_plane(d, carry):
        pl.semaphore_signal(barrier, inc=1, device_id=plane_peer(d)[1], device_id_type=MESH)
        return carry

    lax.fori_loop(1, n_grp, greet_group, 0)
    lax.fori_loop(1, n_pl, greet_plane, 0)

    lane = lax.broadcasted_iota(jnp.int32, (c, tw), 1)
    left = lane == 0
    right = lane == tw - 1
    edge = (tw - 1) * (1 - col)
    edge_row = (1 - rh) * (th - 1)
    is_c1 = col.astype(F32)
    is_c0 = 1.0 - is_c1

    def pack_cols(get):
        def step(h, got):
            turned = pltpu.roll(get(h), (h + tw - edge) % tw, 1)
            return jnp.where(lane == h, turned, got)

        return lax.fori_loop(0, th, step, jnp.zeros((c, tw), F32))

    def halo_copies(k, row_src):
        out = []
        for s, (src, flip) in enumerate(((packed.at[k], 1), (row_src, 2), (row_src, 3))):
            pcol = col if flip == 2 else 1 - col
            prow = rh if flip == 1 else 1 - rh
            out.append(
                pltpu.make_async_remote_copy(
                    src_ref=src, dst_ref=halo.at[k, s], send_sem=h_send.at[k, s], recv_sem=h_recv.at[k, s],
                    device_id={"sp": prow * 2 + pcol, "bn": bn, "dp": dp}, device_id_type=MESH,
                )
            )
        return out

    def fill(dst, k, get):
        got = halo[k, 0].astype(F32)

        def step(h, carry):
            v = get(h)
            edge_col = pltpu.roll(got, (edge + tw - h) % tw, 1)
            dst[h + 1, 0:c] = jnp.where(left, edge_col * is_c1, pltpu.roll(v, 1, 1)).astype(BF16)
            dst[h + 1, c : 2 * c] = v.astype(BF16)
            dst[h + 1, 2 * c : 3 * c] = jnp.where(right, edge_col * is_c0, pltpu.roll(v, tw - 1, 1)).astype(BF16)
            return carry

        lax.fori_loop(0, th, step, 0)
        v = halo[k, 1].astype(F32)
        diag = halo[k, 2].astype(F32)
        real = (1 - rh) * (th + 1)
        dst[real, 0:c] = jnp.where(left, pltpu.roll(diag, 1, 1) * is_c1, pltpu.roll(v, 1, 1)).astype(BF16)
        dst[real, c : 2 * c] = v.astype(BF16)
        dst[real, 2 * c : 3 * c] = jnp.where(
            right, pltpu.roll(diag, tw - 1, 1) * is_c0, pltpu.roll(v, tw - 1, 1)
        ).astype(BF16)
        dst[rh * (th + 1)] = jnp.zeros((3 * c, tw), BF16)

    def exchange(k, first, second, meanwhile):
        n = first.shape[1]
        stats[k, me_g, 0:1, 0:n] = first
        stats[k, me_g, 1:2, 0:n] = second

        def copy_to(d):
            return pltpu.make_async_remote_copy(
                src_ref=stats.at[k, me_g], dst_ref=stats.at[k, me_g],
                send_sem=st_send.at[k, d], recv_sem=st_recv.at[k, d],
                device_id=group_peer(d), device_id_type=MESH,
            )

        def start(d, carry):
            copy_to(d).start()
            return carry

        def finish(d, carry):
            src = (me_g + n_grp - d) % n_grp
            arrival = pltpu.make_async_remote_copy(
                src_ref=stats.at[k, me_g], dst_ref=stats.at[k, src],
                send_sem=st_send.at[k, d], recv_sem=st_recv.at[k, d],
                device_id=group_peer(d), device_id_type=MESH,
            )
            arrival.wait_recv()
            arrival.wait_send()
            return carry

        lax.fori_loop(1, n_grp, start, 0)
        meanwhile()
        lax.fori_loop(1, n_grp, finish, 0)
        firsts = [stats[k, j, 0:1, 0:n] for j in range(n_grp)]
        seconds = [stats[k, j, 1:2, 0:n] for j in range(n_grp)]
        return firsts, seconds

    def moments(k, mean_row, square_row, meanwhile):
        means, squares = exchange(k, mean_row, square_row, meanwhile)
        mean = sum(means[1:], means[0]) / float(n_grp)
        square = sum(squares[1:], squares[0])
        for m in means:
            square = square + local_cells * (m - mean) * (m - mean)
        return mean, square / cells

    def sums(k, first, second, meanwhile):
        a, b = exchange(k, first, second, meanwhile)
        return sum(a[1:], a[0]), sum(b[1:], b[0])

    def row_sum(v):
        return jnp.sum(v.T, axis=0, keepdims=True)

    load_x.wait()

    def widen(raw, out, block):
        def step(j, carry):
            rows = pl.ds(pl.multiple_of(j * block, block), block)
            to = pl.ds(pl.multiple_of(j * block * th, 8), block * th)
            out[to] = raw[rows].astype(F32).reshape(block * th, tw)
            return carry

        lax.fori_loop(0, raw.shape[0] // block, step, 0)

    widen(x_raw, xf, 8)
    get_x = lambda h: xf[pl.ds(h, c, stride=th), :]
    packed[0] = pack_cols(get_x).astype(BF16)
    edge_x[...] = get_x(edge_row).astype(BF16)
    pl.semaphore_wait(barrier, n_grp - 1 + n_pl - 1)
    x_copies = halo_copies(0, edge_x)
    for copy in x_copies:
        copy.start()
    for k in range(9):
        wf_ref[:, k * c : (k + 1) * c] = cw_ref[k]
    load_g.wait()
    widen(g_raw, gf, 8)
    for copy in x_copies:
        copy.wait()
    fill(xs, 0, get_x)

    r4 = pick(th, (4, 2, 1))
    r8 = pick(th, (8, 4, 2, 1))
    r2 = pick(th, (2, 1))

    def columns(src, h, r):
        return jnp.concatenate([src[pl.ds(h + k, 3)].reshape(9 * c, tw) for k in range(r)], axis=1)

    def conv_step(t, got):
        h = t * r4
        res = jnp.dot(wf_ref[...], columns(xs, h, r4), preferred_element_type=F32)
        for k in range(r4):
            piece = res[:, k * tw : (k + 1) * tw]
            a_buf[h + k] = piece
            got = got + piece
        return got

    zero_c = jnp.zeros((c, tw), F32)
    total = lax.fori_loop(0, th // r4, conv_step, zero_c)
    mean_col = jnp.sum(total, axis=1, keepdims=True) / local_cells

    def square_step(h, got):
        d = a_buf[h] - mean_col
        return got + d * d

    sq = lax.fori_loop(0, th, square_step, zero_c)
    gain1 = gain1_ref[...]
    gain3 = gain3_ref[...]

    def prepare():
        wpt_ref[...] = wp_ref[...].astype(F32).T.astype(BF16)
        for k in range(9):
            wb_ref[:, k * c : (k + 1) * c] = cw_ref[8 - k].astype(F32).T.astype(BF16)

    mu1, var1 = moments(0, to_row(mean_col), row_sum(sq), prepare)
    s1 = lax.rsqrt(var1 + norm_floor)
    mu1_c = to_col(mu1)
    s1_c = to_col(s1)
    gain1_c = to_col(gain1)
    shift1_c = to_col(shift1_ref[...])

    acc[...] = jnp.zeros_like(acc)

    def wide_step(t, carry):
        h = t * r2
        parts = []
        for k in range(r2):
            n1 = (a_buf[h + k] - mu1_c) * s1_c
            a_buf[h + k] = n1
            p1 = gain1_c * n1 + shift1_c
            parts.append((p1 * sig(p1)).astype(BF16))
        y = jnp.concatenate(parts, axis=1)
        y_buf[:, pl.ds(pl.multiple_of(h * tw, tw), r2 * tw)] = y
        res = jnp.dot(wpt_ref[...], y, preferred_element_type=F32)
        more = None
        for k in range(r2):
            piece = res[:, k * tw : (k + 1) * tw]
            b_buf[h + k] = piece
            more = piece if more is None else more + piece
        acc[...] += more
        return carry

    lax.fori_loop(0, th // r2, wide_step, 0)
    mean3_col = jnp.sum(acc[...], axis=1, keepdims=True) / local_cells
    sq_rows = []
    for j in range(0, co, c):
        m = jnp.broadcast_to(mean3_col[j : j + c], (c, tw))

        def square3(h, got, j=j, m=m):
            d = b_buf[h, j : j + c] - m
            return got + d * d

        sq_rows.append(row_sum(lax.fori_loop(0, th, square3, zero_c, unroll=2)))

    def slopes():
        def step(h, carry):
            p1 = gain1_c * a_buf[h] + shift1_c
            g = sig(p1)
            e1_buf[h] = g * (1.0 + p1 * (1.0 - g))
            return carry

        lax.fori_loop(0, th, step, 0)

    mu3, var3 = moments(1, to_row(mean3_col), jnp.concatenate(sq_rows, axis=1), slopes)
    s3 = lax.rsqrt(var3 + norm_floor)
    mu3_c = to_col(mu3)
    s3_c = to_col(s3)
    gain3_c = to_col(gain3)
    shift3_c = to_col(shift3_ref[...])

    sum_rows, cross_rows = [], []
    for j in range(0, co, c):
        mu_j = mu3_c[j : j + c]
        s_j = s3_c[j : j + c]
        g_j = gain3_c[j : j + c]
        b_j = shift3_c[j : j + c]

        def out_step(h, got, j=j, mu_j=mu_j, s_j=s_j, g_j=g_j, b_j=b_j):
            n3 = (b_buf[h, j : j + c] - mu_j) * s_j
            p3 = g_j * n3 + b_j
            g = sig(p3)
            e3 = gf[pl.ds(j * th + h, c, stride=th), :] * (g * (1.0 + p3 * (1.0 - g)))
            b_buf[h, j : j + c] = n3
            e3_buf[h, j : j + c] = e3
            return got[0] + e3, got[1] + e3 * n3

        ssum, scross = lax.fori_loop(0, th, out_step, (zero_c, zero_c))
        sum_rows.append(row_sum(ssum))
        cross_rows.append(row_sum(scross))
    local_s3 = jnp.concatenate(sum_rows, axis=1)
    local_q3 = jnp.concatenate(cross_rows, axis=1)
    full_s3, full_q3 = sums(2, local_s3, local_q3, lambda: None)
    coef_a = to_col(gain3 * s3)
    coef_s = to_col(full_s3 / cells)
    coef_q = to_col(full_q3 / cells)

    gpt[...] = jnp.zeros_like(gpt)

    def back_step(t, got):
        h = t * r2
        parts = []
        for k in range(r2):
            pieces = []
            for j in range(0, co, c):
                q = slice(j, j + c)
                db = coef_a[q] * (e3_buf[h + k, q] - coef_s[q] - b_buf[h + k, q] * coef_q[q])
                pieces.append(db.astype(BF16))
            parts.append(jnp.concatenate(pieces, axis=0))
        db = jnp.concatenate(parts, axis=1)
        y = y_buf[:, pl.ds(pl.multiple_of(h * tw, tw), r2 * tw)]
        gpt[...] += lax.dot_general(db, y, NT, preferred_element_type=F32)
        gh = jnp.dot(wp_ref[...], db, preferred_element_type=F32)
        ssum, scross = got
        for k in range(r2):
            n1 = a_buf[h + k]
            e1 = gh[:, k * tw : (k + 1) * tw] * e1_buf[h + k]
            e1_buf[h + k] = e1
            ssum = ssum + e1
            scross = scross + e1 * n1
        return ssum, scross

    ssum, scross = lax.fori_loop(0, th // r2, back_step, (zero_c, zero_c))
    local_s1 = row_sum(ssum)
    local_q1 = row_sum(scross)
    full_s1, full_q1 = sums(3, local_s1, local_q1, lambda: None)
    d_a = to_col(gain1 * s1)
    d_s = to_col(full_s1 / cells)
    d_q = to_col(full_q1 / cells)

    def da_step(h, got):
        da = (d_a * (e1_buf[h] - d_s - a_buf[h] * d_q)).astype(BF16)
        ds[h + 1, c : 2 * c] = da
        turned = pltpu.roll(da.astype(F32), (h + tw - edge) % tw, 1)
        return jnp.where(lane == h, turned, got)

    packed[1] = lax.fori_loop(0, th, da_step, zero_c).astype(BF16)
    d_copies = halo_copies(1, ds.at[edge_row + 1, pl.ds(c, c)])
    for copy in d_copies:
        copy.start()

    cgt[...] = jnp.zeros_like(cgt)

    def grad_step(t, carry):
        h = t * r8
        da = jnp.concatenate([ds[h + k + 1, c : 2 * c] for k in range(r8)], axis=1)
        cgt[...] += lax.dot_general(columns(xs, h, r8), da, NT, preferred_element_type=F32)
        return carry

    lax.fori_loop(0, th // r8, grad_step, 0)
    half = 9 * c // 2
    flat = jnp.concatenate([cgt[k * c : (k + 1) * c, :].T for k in range(9)], axis=0)
    rs_send[0:half] = jnp.concatenate([flat[:half], flat[half:]], axis=1)
    gp = gpt[...].T
    base = half
    for k in range(co // LANES):
        rs_send[base : base + c] = gp[:, k * LANES : (k + 1) * LANES]
        base += c
    rs_send[base:] = jnp.zeros((rs_send.shape[0] - base, LANES), F32)
    rs_send[base : base + 1] = jnp.concatenate([local_q1, local_s1], axis=1)
    small = base + 1
    for v in (local_q3, local_s3):
        for k in range(co // LANES):
            rs_send[small : small + 1] = v[:, k * LANES : (k + 1) * LANES]
            small += 1

    def span(p):
        return pl.ds(pl.multiple_of(p * shard, 8), shard)

    def rs_copy(d):
        p, where = plane_peer(d)
        return pltpu.make_async_remote_copy(
            src_ref=rs_send.at[span(p)], dst_ref=rs_recv.at[d], send_sem=rs_ss.at[d], recv_sem=rs_rs.at[d],
            device_id=where, device_id_type=MESH,
        )

    def rs_start(d, carry):
        rs_copy(d).start()
        return carry

    lax.fori_loop(1, n_pl, rs_start, 0)
    for copy in d_copies:
        copy.wait()

    fill(ds, 1, lambda h: ds[h + 1, c : 2 * c].astype(F32))

    def field_step(t, carry):
        h = t * r4
        res = jnp.dot(wb_ref[...], columns(ds, h, r4), preferred_element_type=F32)
        for k in range(r4):
            ig_ref[h + k] = res[:, k * tw : (k + 1) * tw].astype(BF16)
        return carry


    def rs_wait(d, got):
        rs_copy(d).wait()
        return got + rs_recv[d]

    line[sp] = lax.fori_loop(1, n_pl, rs_wait, rs_send[span(me_p)])

    def ln_copy(d, slot):
        return pltpu.make_async_remote_copy(
            src_ref=line.at[sp], dst_ref=line.at[slot], send_sem=ln_ss.at[d], recv_sem=ln_rs.at[d],
            device_id=line_peer(d), device_id_type=MESH,
        )

    for d in range(1, n_sp):
        ln_copy(d, sp).start()
    middle = th // r4 // 2
    lax.fori_loop(0, middle, field_step, 0)
    for d in range(1, n_sp):
        ln_copy(d, (sp + n_sp - d) % n_sp).wait()
    whole = line[0]
    for k in range(1, n_sp):
        whole = whole + line[k]
    fin[span(me_p)] = whole * factor

    def ag_copy(d, slot):
        return pltpu.make_async_remote_copy(
            src_ref=fin.at[span(me_p)], dst_ref=fin.at[span(slot)], send_sem=ag_ss.at[d], recv_sem=ag_rs.at[d],
            device_id=plane_peer(d)[1], device_id_type=MESH,
        )

    def ag_start(d, carry):
        ag_copy(d, me_p).start()
        return carry

    def ag_wait(d, carry):
        ag_copy(d, (me_p + n_pl - d) % n_pl).wait()
        return carry

    lax.fori_loop(1, n_pl, ag_start, 0)
    lax.fori_loop(middle, th // r4, field_step, 0)
    lax.fori_loop(1, n_pl, ag_wait, 0)


def finish_kernel(ig_in, fin, ig_out, cg_out, pg_out, q1_out, s1_out, q3_out, s3_out, turned):
    th, c, tw = ig_in.shape
    co = pg_out.shape[1]

    def step(h, carry):
        turned[pl.ds(h, c, stride=th), :] = ig_in[h].astype(F32)
        return carry

    lax.fori_loop(0, th, step, 0)
    half = 9 * c // 2
    cg_out[0:half] = fin[0:half, 0:c]
    cg_out[half:] = fin[0:half, c : 2 * c]
    base = half
    for k in range(co // LANES):
        pg_out[:, k * LANES : (k + 1) * LANES] = fin[base : base + c]
        base += c
    q1_out[...] = fin[base : base + 1, 0:c]
    s1_out[...] = fin[base : base + 1, c : 2 * c]
    small = base + 1
    for ref in (q3_out, s3_out):
        for k in range(co // LANES):
            ref[:, k * LANES : (k + 1) * LANES] = fin[small : small + 1]
            small += 1

    def narrow(j, carry):
        rows = pl.ds(pl.multiple_of(j * 8, 8), 8)
        part = turned[pl.ds(pl.multiple_of(j * 8 * th, 8), 8 * th), :]
        ig_out[rows] = part.reshape(8, th, tw).astype(BF16)
        return carry

    lax.fori_loop(0, c // 8, narrow, 0)


def shards(images, out_grad, conv_weight, proj_weight, gain_one, shift_one, gain_three, shift_three):
    _, _, c, th, tw = images.shape
    co = out_grad.shape[2]
    n_sp, n_bn, n_dp = (lax.axis_size(a) for a in ("sp", "bn", "dp"))
    n_grp, n_pl = n_sp * n_bn, n_bn * n_dp
    rows = 9 * c // 2 + c * (co // LANES) + 1 + 2 * (co // LANES)
    shard = 8 * (-(-rows // (8 * n_pl)))
    vm = pl.BlockSpec(memory_space=pltpu.VMEM)
    dma = pltpu.SemaphoreType.DMA
    any_space = pl.BlockSpec(memory_space=pl.ANY)
    ig, fin = pl.pallas_call(
        functools.partial(kernel, n_sp, n_bn, n_dp),
        out_shape=(
            jax.ShapeDtypeStruct((th, c, tw), BF16),
            jax.ShapeDtypeStruct((n_pl * shard, LANES), F32),
        ),
        in_specs=[any_space, any_space] + [vm] * 6,
        out_specs=(vm, vm),
        scratch_shapes=[
            pltpu.VMEM((c, th, tw), BF16),
            pltpu.VMEM((co, th, tw), BF16),
            pltpu.VMEM((c * th, tw), F32),
            pltpu.VMEM((co * th, tw), F32),
            dma, dma,
            pltpu.VMEM((c, 9 * c), BF16),
            pltpu.VMEM((c, 9 * c), BF16),
            pltpu.VMEM((co, c), BF16),
            pltpu.VMEM((th + 2, 3 * c, tw), BF16),
            pltpu.VMEM((th + 2, 3 * c, tw), BF16),
            pltpu.VMEM((th, c, tw), F32),
            pltpu.VMEM((th, c, tw), F32),
            pltpu.VMEM((th, co, tw), F32),
            pltpu.VMEM((th, co, tw), F32),
            pltpu.VMEM((c, th * tw), BF16),
            pltpu.VMEM((co, tw), F32),
            pltpu.VMEM((9 * c, c), F32),
            pltpu.VMEM((co, c), F32),
            pltpu.VMEM((2, c, tw), BF16),
            pltpu.VMEM((c, tw), BF16),
            pltpu.VMEM((2, 3, c, tw), BF16),
            pltpu.VMEM((4, n_grp, 8, co), F32),
            pltpu.VMEM((n_pl * shard, LANES), F32),
            pltpu.VMEM((n_pl, shard, LANES), F32),
            pltpu.VMEM((n_sp, shard, LANES), F32),
            dma((2, 3)), dma((2, 3)),
            dma((4, n_grp)), dma((4, n_grp)),
            dma((n_pl,)), dma((n_pl,)),
            dma((n_sp,)), dma((n_sp,)),
            dma((n_pl,)), dma((n_pl,)),
        ],
        compiler_params=pltpu.CompilerParams(
            collective_id=0, has_side_effects=True, vmem_limit_bytes=60 * 1024 * 1024
        ),
        name="branch_step",
    )(
        images[0, 0], out_grad[0, 0], conv_weight.reshape(9, c, c), proj_weight,
        gain_one[None], shift_one[None], gain_three[None], shift_three[None],
    )
    ig, cg, pg, q1, s1, q3, s3 = pl.pallas_call(
        finish_kernel,
        out_shape=(
            jax.ShapeDtypeStruct((c, th, tw), BF16),
            jax.ShapeDtypeStruct((9 * c, c), F32),
            jax.ShapeDtypeStruct((c, co), F32),
            jax.ShapeDtypeStruct((1, c), F32),
            jax.ShapeDtypeStruct((1, c), F32),
            jax.ShapeDtypeStruct((1, co), F32),
            jax.ShapeDtypeStruct((1, co), F32),
        ),
        in_specs=[vm] * 2,
        out_specs=(vm,) * 7,
        scratch_shapes=[pltpu.VMEM((c * th, tw), F32)],
        name="unpack",
    )(ig, fin)
    return (
        ig[None, None],
        cg.reshape(conv_weight.shape),
        pg, q1[0], s1[0], q3[0], s3[0],
    )


def solution(mesh):
    tiles = P(("bn", "dp"), "sp", None, None, None)
    return jax.shard_map(
        shards,
        mesh=mesh,
        in_specs=(tiles, tiles) + (P(),) * 6,
        out_specs=(tiles,) + (P(),) * 6,
        check_vma=False,
    )
```

```python
import functools

import jax
import jax.numpy as jnp
from jax import lax
from jax.experimental import pallas as pl
from jax.experimental.pallas import tpu as pltpu
from jax.sharding import PartitionSpec as P

norm_floor = 1e-05
F32 = jnp.float32
BF16 = jnp.bfloat16
MESH = pl.DeviceIdType.MESH
LANES = 128
NT = (((1,), (1,)), ((), ()))


def sig(v):
    return 0.5 * jnp.tanh(0.5 * v) + 0.5


def to_row(col):
    return jnp.broadcast_to(col, (col.shape[0], LANES)).T[0:1]


def to_col(row):
    return jnp.broadcast_to(row, (LANES, row.shape[1])).T


def pick(count, options):
    return next(o for o in options if count % o == 0)


def kernel(
    n_sp, n_bn, n_dp,
    x_hbm, g_hbm, cw_ref, wp_ref, gain1_ref, shift1_ref, gain3_ref, shift3_ref,
    ig_ref, fin, vec_out,
    x_raw, g_raw, xf, gf, x_sem, g_sem, wf_ref, wb_ref, wpt_ref,
    xs, ds, a_buf, e1_buf, b_buf, e3_buf, y_buf, acc, cgt, gpt,
    packed, edge_x, halo, stats, rs_send, rs_recv, line, vec,
    h_send, h_recv, st_send, st_recv, rs_ss, rs_rs, ln_ss, ln_rs, ag_ss, ag_rs, vec_ss, vec_rs,
):
    c, th, tw = x_raw.shape
    co = g_raw.shape[0]
    n_grp = n_sp * n_bn
    n_pl = n_bn * n_dp
    shard = line.shape[1]
    local_cells = float(th * tw)
    cells = local_cells * n_grp
    factor = 1.0 / (n_sp * local_cells)
    sp = lax.axis_index("sp")
    bn = lax.axis_index("bn")
    dp = lax.axis_index("dp")
    col = sp % 2
    rh = sp // 2
    me_g = sp * n_bn + bn
    me_p = bn * n_dp + dp

    def group_peer(d):
        p = (me_g + d) % n_grp
        return {"sp": p // n_bn, "bn": p % n_bn, "dp": dp}

    def plane_peer(d):
        p = (me_p + d) % n_pl
        return p, {"sp": sp, "bn": p // n_dp, "dp": p % n_dp}

    def line_peer(d):
        return {"sp": (sp + d) % n_sp, "bn": bn, "dp": dp}

    load_x = pltpu.make_async_copy(x_hbm, x_raw, x_sem)
    load_g = pltpu.make_async_copy(g_hbm, g_raw, g_sem)
    load_x.start()
    load_g.start()

    barrier = pltpu.get_barrier_semaphore()

    def greet_group(d, carry):
        pl.semaphore_signal(barrier, inc=1, device_id=group_peer(d), device_id_type=MESH)
        return carry

    def greet_plane(d, carry):
        pl.semaphore_signal(barrier, inc=1, device_id=plane_peer(d)[1], device_id_type=MESH)
        return carry

    lax.fori_loop(1, n_grp, greet_group, 0)
    lax.fori_loop(1, n_pl, greet_plane, 0)

    lane = lax.broadcasted_iota(jnp.int32, (c, tw), 1)
    left = lane == 0
    right = lane == tw - 1
    edge = (tw - 1) * (1 - col)
    edge_row = (1 - rh) * (th - 1)
    is_c1 = col.astype(F32)
    is_c0 = 1.0 - is_c1

    def pack_cols(get):
        def step(h, got):
            turned = pltpu.roll(get(h), (h + tw - edge) % tw, 1)
            return jnp.where(lane == h, turned, got)

        return lax.fori_loop(0, th, step, jnp.zeros((c, tw), F32))

    def halo_copies(k, row_src):
        out = []
        for s, (src, flip) in enumerate(((packed.at[k], 1), (row_src, 2), (row_src, 3))):
            pcol = col if flip == 2 else 1 - col
            prow = rh if flip == 1 else 1 - rh
            out.append(
                pltpu.make_async_remote_copy(
                    src_ref=src, dst_ref=halo.at[k, s], send_sem=h_send.at[k, s], recv_sem=h_recv.at[k, s],
                    device_id={"sp": prow * 2 + pcol, "bn": bn, "dp": dp}, device_id_type=MESH,
                )
            )
        return out

    def fill(dst, k, get):
        got = halo[k, 0].astype(F32)

        def step(h, carry):
            v = get(h)
            edge_col = pltpu.roll(got, (edge + tw - h) % tw, 1)
            dst[h + 1, 0:c] = jnp.where(left, edge_col * is_c1, pltpu.roll(v, 1, 1)).astype(BF16)
            dst[h + 1, c : 2 * c] = v.astype(BF16)
            dst[h + 1, 2 * c : 3 * c] = jnp.where(right, edge_col * is_c0, pltpu.roll(v, tw - 1, 1)).astype(BF16)
            return carry

        lax.fori_loop(0, th, step, 0)
        v = halo[k, 1].astype(F32)
        diag = halo[k, 2].astype(F32)
        real = (1 - rh) * (th + 1)
        dst[real, 0:c] = jnp.where(left, pltpu.roll(diag, 1, 1) * is_c1, pltpu.roll(v, 1, 1)).astype(BF16)
        dst[real, c : 2 * c] = v.astype(BF16)
        dst[real, 2 * c : 3 * c] = jnp.where(
            right, pltpu.roll(diag, tw - 1, 1) * is_c0, pltpu.roll(v, tw - 1, 1)
        ).astype(BF16)
        dst[rh * (th + 1)] = jnp.zeros((3 * c, tw), BF16)

    def exchange(k, first, second, meanwhile):
        n = first.shape[1]
        both = jnp.concatenate([first, second], axis=1)
        used = 2 * n // LANES
        for r in range(used):
            stats[k, me_g, r : r + 1] = both[:, r * LANES : (r + 1) * LANES]
        rows = pl.ds(0, used)

        def copy_to(d):
            return pltpu.make_async_remote_copy(
                src_ref=stats.at[k, me_g, rows], dst_ref=stats.at[k, me_g, rows],
                send_sem=st_send.at[k, d], recv_sem=st_recv.at[k, d],
                device_id=group_peer(d), device_id_type=MESH,
            )

        def start(d, carry):
            copy_to(d).start()
            return carry

        def finish(d, carry):
            src = (me_g + n_grp - d) % n_grp
            arrival = pltpu.make_async_remote_copy(
                src_ref=stats.at[k, me_g, rows], dst_ref=stats.at[k, src, rows],
                send_sem=st_send.at[k, d], recv_sem=st_recv.at[k, d],
                device_id=group_peer(d), device_id_type=MESH,
            )
            arrival.wait_recv()
            arrival.wait_send()
            return carry

        lax.fori_loop(1, n_grp, start, 0)
        meanwhile()
        lax.fori_loop(1, n_grp, finish, 0)
        firsts, seconds = [], []
        for j in range(n_grp):
            flat = jnp.concatenate([stats[k, j, r : r + 1] for r in range(used)], axis=1)
            firsts.append(flat[:, :n])
            seconds.append(flat[:, n:])
        return firsts, seconds

    def moments(k, mean_row, square_row, meanwhile):
        means, squares = exchange(k, mean_row, square_row, meanwhile)
        mean = sum(means[1:], means[0]) / float(n_grp)
        square = sum(squares[1:], squares[0])
        for m in means:
            square = square + local_cells * (m - mean) * (m - mean)
        return mean, square / cells

    def sums(k, first, second, meanwhile):
        a, b = exchange(k, first, second, meanwhile)
        return sum(a[1:], a[0]), sum(b[1:], b[0])

    def row_sum(v):
        return jnp.sum(v.T, axis=0, keepdims=True)

    load_x.wait()

    def widen(raw, out, block):
        def step(j, carry):
            rows = pl.ds(pl.multiple_of(j * block, block), block)
            to = pl.ds(pl.multiple_of(j * block * th, 8), block * th)
            out[to] = raw[rows].astype(F32).reshape(block * th, tw)
            return carry

        lax.fori_loop(0, raw.shape[0] // block, step, 0)

    widen(x_raw, xf, 8)
    get_x = lambda h: xf[pl.ds(h, c, stride=th), :]
    packed[0] = pack_cols(get_x).astype(BF16)
    edge_x[...] = get_x(edge_row).astype(BF16)
    pl.semaphore_wait(barrier, n_grp - 1 + n_pl - 1)
    x_copies = halo_copies(0, edge_x)
    for copy in x_copies:
        copy.start()
    for k in range(9):
        wf_ref[:, k * c : (k + 1) * c] = cw_ref[k]
    load_g.wait()
    widen(g_raw, gf, 8)
    for copy in x_copies:
        copy.wait()
    fill(xs, 0, get_x)

    r4 = pick(th, (4, 2, 1))
    r8 = pick(th, (8, 4, 2, 1))
    r2 = pick(th, (2, 1))

    def columns(src, h, r):
        return jnp.concatenate([src[pl.ds(h + k, 3)].reshape(9 * c, tw) for k in range(r)], axis=1)

    def conv_step(t, got):
        h = t * r4
        res = jnp.dot(wf_ref[...], columns(xs, h, r4), preferred_element_type=F32)
        for k in range(r4):
            piece = res[:, k * tw : (k + 1) * tw]
            a_buf[h + k] = piece
            got = got + piece
        return got

    zero_c = jnp.zeros((c, tw), F32)
    total = lax.fori_loop(0, th // r4, conv_step, zero_c)
    mean_col = jnp.sum(total, axis=1, keepdims=True) / local_cells

    def square_step(h, got):
        d = a_buf[h] - mean_col
        return got + d * d

    sq = lax.fori_loop(0, th, square_step, zero_c)
    gain1 = gain1_ref[...]
    gain3 = gain3_ref[...]

    def prepare():
        wpt_ref[...] = wp_ref[...].astype(F32).T.astype(BF16)
        for k in range(9):
            wb_ref[:, k * c : (k + 1) * c] = cw_ref[8 - k].astype(F32).T.astype(BF16)

    mu1, var1 = moments(0, to_row(mean_col), row_sum(sq), prepare)
    s1 = lax.rsqrt(var1 + norm_floor)
    mu1_c = to_col(mu1)
    s1_c = to_col(s1)
    gain1_c = to_col(gain1)
    shift1_c = to_col(shift1_ref[...])

    acc[...] = jnp.zeros_like(acc)

    def wide_step(t, carry):
        h = t * r2
        parts = []
        for k in range(r2):
            n1 = (a_buf[h + k] - mu1_c) * s1_c
            a_buf[h + k] = n1
            p1 = gain1_c * n1 + shift1_c
            parts.append((p1 * sig(p1)).astype(BF16))
        y = jnp.concatenate(parts, axis=1)
        y_buf[:, pl.ds(pl.multiple_of(h * tw, tw), r2 * tw)] = y
        res = jnp.dot(wpt_ref[...], y, preferred_element_type=F32)
        more = None
        for k in range(r2):
            piece = res[:, k * tw : (k + 1) * tw]
            b_buf[h + k] = piece
            more = piece if more is None else more + piece
        acc[...] += more
        return carry

    lax.fori_loop(0, th // r2, wide_step, 0)
    mean3_col = jnp.sum(acc[...], axis=1, keepdims=True) / local_cells
    sq_rows = []
    for j in range(0, co, c):
        m = jnp.broadcast_to(mean3_col[j : j + c], (c, tw))

        def square3(h, got, j=j, m=m):
            d = b_buf[h, j : j + c] - m
            return got + d * d

        sq_rows.append(row_sum(lax.fori_loop(0, th, square3, zero_c, unroll=2)))

    def slopes():
        def step(h, carry):
            p1 = gain1_c * a_buf[h] + shift1_c
            g = sig(p1)
            e1_buf[h] = g * (1.0 + p1 * (1.0 - g))
            return carry

        lax.fori_loop(0, th, step, 0)

    mu3, var3 = moments(1, to_row(mean3_col), jnp.concatenate(sq_rows, axis=1), slopes)
    s3 = lax.rsqrt(var3 + norm_floor)
    mu3_c = to_col(mu3)
    s3_c = to_col(s3)
    gain3_c = to_col(gain3)
    shift3_c = to_col(shift3_ref[...])

    sum_rows, cross_rows = [], []
    for j in range(0, co, c):
        mu_j = mu3_c[j : j + c]
        s_j = s3_c[j : j + c]
        g_j = gain3_c[j : j + c]
        b_j = shift3_c[j : j + c]

        def out_step(h, got, j=j, mu_j=mu_j, s_j=s_j, g_j=g_j, b_j=b_j):
            n3 = (b_buf[h, j : j + c] - mu_j) * s_j
            p3 = g_j * n3 + b_j
            g = sig(p3)
            e3 = gf[pl.ds(j * th + h, c, stride=th), :] * (g * (1.0 + p3 * (1.0 - g)))
            b_buf[h, j : j + c] = n3
            e3_buf[h, j : j + c] = e3
            return got[0] + e3, got[1] + e3 * n3

        ssum, scross = lax.fori_loop(0, th, out_step, (zero_c, zero_c))
        sum_rows.append(row_sum(ssum))
        cross_rows.append(row_sum(scross))
    local_s3 = jnp.concatenate(sum_rows, axis=1)
    local_q3 = jnp.concatenate(cross_rows, axis=1)
    full_s3, full_q3 = sums(2, local_s3, local_q3, lambda: None)
    coef_a = to_col(gain3 * s3)
    coef_s = to_col(full_s3 / cells)
    coef_q = to_col(full_q3 / cells)

    gpt[...] = jnp.zeros_like(gpt)

    def back_step(t, got):
        h = t * r2
        parts = []
        for k in range(r2):
            pieces = []
            for j in range(0, co, c):
                q = slice(j, j + c)
                db = coef_a[q] * (e3_buf[h + k, q] - coef_s[q] - b_buf[h + k, q] * coef_q[q])
                pieces.append(db.astype(BF16))
            parts.append(jnp.concatenate(pieces, axis=0))
        db = jnp.concatenate(parts, axis=1)
        y = y_buf[:, pl.ds(pl.multiple_of(h * tw, tw), r2 * tw)]
        gpt[...] += lax.dot_general(db, y, NT, preferred_element_type=F32)
        gh = jnp.dot(wp_ref[...], db, preferred_element_type=F32)
        ssum, scross = got
        for k in range(r2):
            n1 = a_buf[h + k]
            e1 = gh[:, k * tw : (k + 1) * tw] * e1_buf[h + k]
            e1_buf[h + k] = e1
            ssum = ssum + e1
            scross = scross + e1 * n1
        return ssum, scross

    ssum, scross = lax.fori_loop(0, th // r2, back_step, (zero_c, zero_c))
    local_s1 = row_sum(ssum)
    local_q1 = row_sum(scross)
    full_s1, full_q1 = sums(3, local_s1, local_q1, lambda: None)
    vec[dp] = jnp.zeros(vec.shape[1:], F32)
    flat_vec = jnp.concatenate([full_q1, full_s1, full_q3, full_s3], axis=1)
    n_vec = flat_vec.shape[1] // LANES
    for r in range(n_vec):
        vec[dp, r : r + 1] = flat_vec[:, r * LANES : (r + 1) * LANES]

    def vec_copy(d, slot):
        return pltpu.make_async_remote_copy(
            src_ref=vec.at[dp], dst_ref=vec.at[slot], send_sem=vec_ss.at[d], recv_sem=vec_rs.at[d],
            device_id={"sp": sp, "bn": bn, "dp": (dp + d) % n_dp}, device_id_type=MESH,
        )

    for d in range(1, n_dp):
        vec_copy(d, dp).start()
    d_a = to_col(gain1 * s1)
    d_s = to_col(full_s1 / cells)
    d_q = to_col(full_q1 / cells)

    def da_step(h, got):
        da = (d_a * (e1_buf[h] - d_s - a_buf[h] * d_q)).astype(BF16)
        ds[h + 1, c : 2 * c] = da
        turned = pltpu.roll(da.astype(F32), (h + tw - edge) % tw, 1)
        return jnp.where(lane == h, turned, got)

    packed[1] = lax.fori_loop(0, th, da_step, zero_c).astype(BF16)
    d_copies = halo_copies(1, ds.at[edge_row + 1, pl.ds(c, c)])
    for copy in d_copies:
        copy.start()

    cgt[...] = jnp.zeros_like(cgt)

    def grad_step(t, carry):
        h = t * r8
        da = jnp.concatenate([ds[h + k + 1, c : 2 * c] for k in range(r8)], axis=1)
        cgt[...] += lax.dot_general(columns(xs, h, r8), da, NT, preferred_element_type=F32)
        return carry

    lax.fori_loop(0, th // r8, grad_step, 0)
    half = 9 * c // 2
    flat = jnp.concatenate([cgt[k * c : (k + 1) * c, :].T for k in range(9)], axis=0)
    rs_send[0:half] = jnp.concatenate([flat[:half], flat[half:]], axis=1).astype(BF16)
    gp = gpt[...].T
    base = half
    for k in range(co // LANES):
        rs_send[base : base + c] = gp[:, k * LANES : (k + 1) * LANES].astype(BF16)
        base += c
    if base < rs_send.shape[0]:
        rs_send[base:] = jnp.zeros((rs_send.shape[0] - base, LANES), BF16)

    def span(p):
        return pl.ds(pl.multiple_of(p * shard, 16), shard)

    def rs_copy(d):
        p, where = plane_peer(d)
        return pltpu.make_async_remote_copy(
            src_ref=rs_send.at[span(p)], dst_ref=rs_recv.at[d], send_sem=rs_ss.at[d], recv_sem=rs_rs.at[d],
            device_id=where, device_id_type=MESH,
        )

    def rs_start(d, carry):
        rs_copy(d).start()
        return carry

    lax.fori_loop(1, n_pl, rs_start, 0)
    for copy in d_copies:
        copy.wait()

    fill(ds, 1, lambda h: ds[h + 1, c : 2 * c].astype(F32))

    def field_step(t, carry):
        h = t * r4
        res = jnp.dot(wb_ref[...], columns(ds, h, r4), preferred_element_type=F32)
        for k in range(r4):
            ig_ref[h + k] = res[:, k * tw : (k + 1) * tw].astype(BF16)
        return carry


    def rs_wait(d, got):
        rs_copy(d).wait()
        return got + rs_recv[d].astype(F32)

    line[sp] = lax.fori_loop(1, n_pl, rs_wait, rs_send[span(me_p)].astype(F32)).astype(BF16)

    def ln_copy(d, slot):
        return pltpu.make_async_remote_copy(
            src_ref=line.at[sp], dst_ref=line.at[slot], send_sem=ln_ss.at[d], recv_sem=ln_rs.at[d],
            device_id=line_peer(d), device_id_type=MESH,
        )

    for d in range(1, n_sp):
        ln_copy(d, sp).start()
    middle = th // r4 // 2
    lax.fori_loop(0, middle, field_step, 0)
    for d in range(1, n_sp):
        ln_copy(d, (sp + n_sp - d) % n_sp).wait()
    whole = line[0].astype(F32)
    for k in range(1, n_sp):
        whole = whole + line[k].astype(F32)
    fin[span(me_p)] = (whole * factor).astype(BF16)

    def ag_copy(d, slot):
        return pltpu.make_async_remote_copy(
            src_ref=fin.at[span(me_p)], dst_ref=fin.at[span(slot)], send_sem=ag_ss.at[d], recv_sem=ag_rs.at[d],
            device_id=plane_peer(d)[1], device_id_type=MESH,
        )

    def ag_start(d, carry):
        ag_copy(d, me_p).start()
        return carry

    def ag_wait(d, carry):
        ag_copy(d, (me_p + n_pl - d) % n_pl).wait()
        return carry

    lax.fori_loop(1, n_pl, ag_start, 0)
    lax.fori_loop(middle, th // r4, field_step, 0)
    lax.fori_loop(1, n_pl, ag_wait, 0)
    for d in range(1, n_dp):
        vec_copy(d, (dp + n_dp - d) % n_dp).wait()
    vec_sum = vec[0]
    for k in range(1, n_dp):
        vec_sum = vec_sum + vec[k]
    vec_out[...] = vec_sum * factor


def finish_kernel(ig_in, fin, vec, ig_out, cg_out, pg_out, q1_out, s1_out, q3_out, s3_out, turned):
    th, c, tw = ig_in.shape
    co = pg_out.shape[1]

    def step(h, carry):
        turned[pl.ds(h, c, stride=th), :] = ig_in[h].astype(F32)
        return carry

    lax.fori_loop(0, th, step, 0)
    half = 9 * c // 2
    cg_out[0:half] = fin[0:half, 0:c].astype(F32)
    cg_out[half:] = fin[0:half, c : 2 * c].astype(F32)
    base = half
    for k in range(co // LANES):
        pg_out[:, k * LANES : (k + 1) * LANES] = fin[base : base + c].astype(F32)
        base += c
    q1_out[...] = vec[0:1, 0:c]
    s1_out[...] = vec[0:1, c : 2 * c]
    small = 1
    for ref in (q3_out, s3_out):
        for k in range(co // LANES):
            ref[:, k * LANES : (k + 1) * LANES] = vec[small : small + 1]
            small += 1

    def narrow(j, carry):
        rows = pl.ds(pl.multiple_of(j * 8, 8), 8)
        part = turned[pl.ds(pl.multiple_of(j * 8 * th, 8), 8 * th), :]
        ig_out[rows] = part.reshape(8, th, tw).astype(BF16)
        return carry

    lax.fori_loop(0, c // 8, narrow, 0)


def shards(images, out_grad, conv_weight, proj_weight, gain_one, shift_one, gain_three, shift_three):
    _, _, c, th, tw = images.shape
    co = out_grad.shape[2]
    n_sp, n_bn, n_dp = (lax.axis_size(a) for a in ("sp", "bn", "dp"))
    n_grp, n_pl = n_sp * n_bn, n_bn * n_dp
    rows = 9 * c // 2 + c * (co // LANES)
    shard = 16 * (-(-rows // (16 * n_pl)))
    vec_rows = 8 * (-(-(2 * c + 2 * co) // (8 * LANES)))
    vm = pl.BlockSpec(memory_space=pltpu.VMEM)
    dma = pltpu.SemaphoreType.DMA
    any_space = pl.BlockSpec(memory_space=pl.ANY)
    ig, fin, vec = pl.pallas_call(
        functools.partial(kernel, n_sp, n_bn, n_dp),
        out_shape=(
            jax.ShapeDtypeStruct((th, c, tw), BF16),
            jax.ShapeDtypeStruct((n_pl * shard, LANES), BF16),
            jax.ShapeDtypeStruct((vec_rows, LANES), F32),
        ),
        in_specs=[any_space, any_space] + [vm] * 6,
        out_specs=(vm,) * 3,
        scratch_shapes=[
            pltpu.VMEM((c, th, tw), BF16),
            pltpu.VMEM((co, th, tw), BF16),
            pltpu.VMEM((c * th, tw), F32),
            pltpu.VMEM((co * th, tw), F32),
            dma, dma,
            pltpu.VMEM((c, 9 * c), BF16),
            pltpu.VMEM((c, 9 * c), BF16),
            pltpu.VMEM((co, c), BF16),
            pltpu.VMEM((th + 2, 3 * c, tw), BF16),
            pltpu.VMEM((th + 2, 3 * c, tw), BF16),
            pltpu.VMEM((th, c, tw), F32),
            pltpu.VMEM((th, c, tw), F32),
            pltpu.VMEM((th, co, tw), F32),
            pltpu.VMEM((th, co, tw), F32),
            pltpu.VMEM((c, th * tw), BF16),
            pltpu.VMEM((co, tw), F32),
            pltpu.VMEM((9 * c, c), F32),
            pltpu.VMEM((co, c), F32),
            pltpu.VMEM((2, c, tw), BF16),
            pltpu.VMEM((c, tw), BF16),
            pltpu.VMEM((2, 3, c, tw), BF16),
            pltpu.VMEM((4, n_grp, max(8, 2 * co // LANES), LANES), F32),
            pltpu.VMEM((n_pl * shard, LANES), BF16),
            pltpu.VMEM((n_pl, shard, LANES), BF16),
            pltpu.VMEM((n_sp, shard, LANES), BF16),
            pltpu.VMEM((n_dp, vec_rows, LANES), F32),
            dma((2, 3)), dma((2, 3)),
            dma((4, n_grp)), dma((4, n_grp)),
            dma((n_pl,)), dma((n_pl,)),
            dma((n_sp,)), dma((n_sp,)),
            dma((n_pl,)), dma((n_pl,)),
            dma((n_dp,)), dma((n_dp,)),
        ],
        compiler_params=pltpu.CompilerParams(
            collective_id=0, has_side_effects=True, vmem_limit_bytes=60 * 1024 * 1024
        ),
        name="branch_step",
    )(
        images[0, 0], out_grad[0, 0], conv_weight.reshape(9, c, c), proj_weight,
        gain_one[None], shift_one[None], gain_three[None], shift_three[None],
    )
    ig, cg, pg, q1, s1, q3, s3 = pl.pallas_call(
        finish_kernel,
        out_shape=(
            jax.ShapeDtypeStruct((c, th, tw), BF16),
            jax.ShapeDtypeStruct((9 * c, c), F32),
            jax.ShapeDtypeStruct((c, co), F32),
            jax.ShapeDtypeStruct((1, c), F32),
            jax.ShapeDtypeStruct((1, c), F32),
            jax.ShapeDtypeStruct((1, co), F32),
            jax.ShapeDtypeStruct((1, co), F32),
        ),
        in_specs=[vm] * 3,
        out_specs=(vm,) * 7,
        scratch_shapes=[pltpu.VMEM((c * th, tw), F32)],
        name="unpack",
    )(ig, fin, vec)
    return (
        ig[None, None],
        cg.reshape(conv_weight.shape),
        pg, q1[0], s1[0], q3[0], s3[0],
    )


def solution(mesh):
    tiles = P(("bn", "dp"), "sp", None, None, None)
    return jax.shard_map(
        shards,
        mesh=mesh,
        in_specs=(tiles, tiles) + (P(),) * 6,
        out_specs=(tiles,) + (P(),) * 6,
        check_vma=False,
    )
```
